32 devices in a mesh: dp: 8 (over z, x), tensor: 4 (over y, core).
Axes of the slice: x: 2, y: 2, z: 4, core: 2. Of those that a mesh axis runs over, the one named last changes fastest.
Arguments:
- inputs: bfloat16 [8192, 2048], P(('dp', 'tensor')), may hold values from -6 to 6
- segment_ids: int32 [8192], P('dp'), may hold values from 0 to 8191, as said below
- w_query: bfloat16 [2048, 2048], P('dp', 'tensor'), may hold values from -0.125 to 0.125
- w_key: bfloat16 [2048, 2048], P('dp', 'tensor'), may hold values from -0.125 to 0.125
- w_value: bfloat16 [2048, 2048], P('dp', 'tensor'), may hold values from -0.125 to 0.125
- w_out: bfloat16 [2048, 2048], P('tensor', 'dp'), may hold values from -0.125 to 0.125
- w_gate: bfloat16 [2048, 8192], P('dp', 'tensor'), may hold values from -0.125 to 0.125
- w_up: bfloat16 [2048, 8192], P('dp', 'tensor'), may hold values from -0.125 to 0.125
- w_down: bfloat16 [8192, 2048], P('tensor', 'dp'), may hold values from -0.0625 to 0.0625
- gain_query: float32 [2048], replicated, may hold values from 0.5 to 2.5
- gain_key: float32 [2048], replicated, may hold values from 0.5 to 2.5
- gain_attn: float32 [2048], replicated, may hold values from 0.1 to 1.9
- gain_mlp: float32 [2048], replicated, may hold values from 0.1 to 1.9
- cotangent: bfloat16 [8192, 2048], P(('dp', 'tensor')), may hold values from -6 to 6
Outputs:
- output: bfloat16 [8192, 2048], P(('dp', 'tensor'))
- grad_inputs: float32 [8192, 2048], P(('dp', 'tensor'))
- grad_query: float32 [2048, 2048], P('dp', 'tensor')
- grad_key: float32 [2048, 2048], P('dp', 'tensor')
- grad_value: float32 [2048, 2048], P('dp', 'tensor')
- grad_out: float32 [2048, 2048], P('tensor', 'dp')
- grad_gate: float32 [2048, 8192], P('dp', 'tensor')
- grad_up: float32 [2048, 8192], P('dp', 'tensor')
- grad_down: float32 [8192, 2048], P('tensor', 'dp')
- grad_gain_query: float32 [2048], replicated
- grad_gain_key: float32 [2048], replicated
- grad_gain_attn: float32 [2048], replicated
- grad_gain_mlp: float32 [2048], replicated
The draws below stay inside these ranges and needn't reach their ends.
Inputs may be any that keep to these rules, and one draw needn't show every extreme that they name: `segment_ids`: segment ids never fall along the 1024 tokens of one group, and no segment crosses from one group into the next; in every draw one group is a single segment of 1024 tokens.
All inputs are finite; a program needn't handle non-finite values.
Results may differ from the reference program's by a relative error of at most 0.015.
The reference program's roundings to bfloat16 on the way count: a program that leaves them out, or rounds other values in their place, can miss the bound.
Values may be sent and summed in bfloat16 or wider, within the bound.
No kernel may reach another device: no remote copies, remote signals or barrier semaphores. Data moves between devices by JAX's collectives and lax.ppermute only.
A program may use at most 192 MiB of HBM per device.

```python
import math
import jax
import jax.numpy as jnp
from jax import lax

D = 2048
HEADS = 16
HEAD_DIM = 128
FF = 8192
TOK_GRP = 1024
TOKENS = 8192


def draw_segment_ids(key, part):
    groups = TOKENS // TOK_GRP
    rate_key = jax.random.fold_in(key, 11)
    boundary_key = jax.random.fold_in(key, 12)
    pick_key = jax.random.fold_in(key, 13)
    levels = jax.random.randint(rate_key, (groups, 1), 5, 10)
    spread = jnp.power(jnp.full((groups, 1), 2, jnp.int32), levels)
    boundary = jax.random.randint(boundary_key, (groups, TOK_GRP), 0, 1 << 20) % spread == 0
    single_group = jax.random.randint(pick_key, (), 0, groups)
    group_index = jnp.arange(groups, dtype=jnp.int32)[:, None]
    column = jnp.arange(TOK_GRP, dtype=jnp.int32)[None, :]
    boundary = boundary & (column > 0) & (group_index != single_group)
    local_ids = jnp.cumsum(boundary.astype(jnp.int32), axis=1)
    return (local_ids + group_index * TOK_GRP).reshape(TOKENS).astype(jnp.int32)


def shard_levels(stream_key, dims, split, low, largest):
    level = 1.0
    for dim, shards_of in split:
        heights = jax.random.uniform(jax.random.fold_in(jax.random.fold_in(stream_key, 6), dim), (shards_of,), jnp.float32, low / len(split), largest / len(split))
        level = level * jnp.repeat(jnp.exp(heights), dims[dim] // shards_of).reshape((-1,) + (1,) * (len(dims) - 1 - dim))
    return level


def gaussian(stream_key, extent, scale, limit, cuts=(), held_as=jnp.bfloat16):
    values = jax.random.normal(stream_key, extent, jnp.float32) * scale
    if len(cuts) > 0:
        values = shard_levels(stream_key, extent, cuts, -0.22, 0.18) * values
    return jnp.clip(values, min=-limit, max=limit).astype(held_as)


def setup_inputs(seed: int = 0) -> dict:
    seeds = jax.random.split(jax.random.key(seed), 15)
    inputs = gaussian(seeds[0], (TOKENS, D), 1.0, 6.0, ((0, 32),))
    segment_ids = draw_segment_ids(jax.random.fold_in(seeds[14], 71), 0)
    w_query = gaussian(seeds[2], (D, D), D ** -0.5, 0.125, ((0, 8), (1, 4)))
    w_key = gaussian(seeds[3], (D, D), D ** -0.5, 0.125, ((0, 8), (1, 4)))
    w_value = gaussian(seeds[4], (D, D), D ** -0.5, 0.125, ((0, 8), (1, 4)))
    w_out = gaussian(seeds[5], (D, D), D ** -0.5, 0.125, ((0, 4), (1, 8)))
    w_gate = gaussian(seeds[6], (D, FF), D ** -0.5, 0.125, ((0, 8), (1, 4)))
    w_up = gaussian(seeds[7], (D, FF), D ** -0.5, 0.125, ((0, 8), (1, 4)))
    w_down = gaussian(seeds[8], (FF, D), FF ** -0.5, 0.0625, ((0, 4), (1, 8)))
    gain_query = jnp.clip(jnp.exp(jax.random.uniform(seeds[9], (D,), jnp.float32, math.log(0.5), math.log(2.5))), 0.5, 2.5)
    gain_key = jnp.clip(jnp.exp(jax.random.uniform(seeds[10], (D,), jnp.float32, math.log(0.5), math.log(2.5))), 0.5, 2.5)
    gain_attn = jnp.clip(1.0 + 0.18 * jax.random.normal(seeds[11], (D,), jnp.float32), 0.1, 1.9)
    gain_mlp = jnp.clip(1.0 + 0.18 * jax.random.normal(seeds[12], (D,), jnp.float32), 0.1, 1.9)
    cotangent = gaussian(seeds[13], (TOKENS, D), 1.0, 6.0, ((0, 32),))
    return {"inputs": inputs, "segment_ids": segment_ids, "w_query": w_query, "w_key": w_key, "w_value": w_value, "w_out": w_out, "w_gate": w_gate, "w_up": w_up, "w_down": w_down, "gain_query": gain_query, "gain_key": gain_key, "gain_attn": gain_attn, "gain_mlp": gain_mlp, "cotangent": cotangent}


EPSILON = 1e-06
THETA_BASE = 500000.0
HIGHEST = lax.Precision.HIGHEST

@jax.custom_vjp
def low(v):
    return lax.optimization_barrier(v.astype(jnp.bfloat16)).astype(jnp.float32)

@jax.custom_vjp
def low_back(v):
    return v

def low_keep(v):
    return (low(v), None)

def low_pass(kept, grad):
    return (grad,)

def back_keep(v):
    return (v, None)

def back_low(kept, grad):
    return (low(grad),)
low.defvjp(low_keep, low_pass)
low_back.defvjp(back_keep, back_low)

def matmul(left, right):
    return jnp.dot(left, right, precision=HIGHEST, preferred_element_type=jnp.float32)

def rms_norm(vector, gain):
    return vector * lax.rsqrt(lax.optimization_barrier(jnp.mean(vector * vector, axis=-1, keepdims=True)) + EPSILON) * gain

def positions(segment):
    earlier = (segment[None, :] < segment[:, None]).astype(jnp.int32)
    return jnp.arange(segment.shape[0], dtype=jnp.int32) - lax.optimization_barrier(jnp.sum(earlier, axis=1)).astype(jnp.int32)

def rope_tables(position, half_dim):
    frequency = THETA_BASE ** (-jnp.arange(half_dim, dtype=jnp.float32) / half_dim)
    angles = position.astype(jnp.float32)[:, None] * frequency[None, :]
    return (jnp.cos(angles), jnp.sin(angles))

def rotate(vectors, cosine, sine_table, direction):
    half_dim = vectors.shape[-1] // 2
    front_half = vectors[..., :half_dim]
    back_half = vectors[..., half_dim:]
    cosine_part = cosine[:, None, :]
    sine_part = sine_table[:, None, :] * direction
    return jnp.concatenate([front_half * cosine_part - back_half * sine_part, back_half * cosine_part + front_half * sine_part], axis=-1)

def group_forward(inputs, segment, params):
    w_query, w_key, w_value, w_out, w_gate, w_up, w_down, gain_query, gain_key, gain_attn, gain_mlp = params
    tokens = inputs.shape[0]
    score_scale = HEAD_DIM ** (-0.5)
    position = positions(segment)
    cosine, sine_table = rope_tables(position, HEAD_DIM // 2)
    token_order = jnp.arange(tokens, dtype=jnp.int32)
    allowed = (segment[None, :] == segment[:, None]) & (token_order[None, :] <= token_order[:, None])
    query_raw = low_back(matmul(inputs, w_query))
    key_raw = low_back(matmul(inputs, w_key))
    value_rows = low(low_back(matmul(inputs, w_value))).reshape(tokens, HEADS, HEAD_DIM)
    query_rot = low(rotate(rms_norm(query_raw, gain_query).reshape(tokens, HEADS, HEAD_DIM), cosine, sine_table, 1.0))
    key_rot = low(rotate(rms_norm(key_raw, gain_key).reshape(tokens, HEADS, HEAD_DIM), cosine, sine_table, 1.0))
    scores = low_back(jnp.einsum('qhd,khd->hqk', query_rot, key_rot, precision=HIGHEST) * score_scale)
    scores = jnp.where(allowed[None, :, :], scores, -1e+30)
    soft_weights = low(jax.nn.softmax(scores, axis=-1))
    attended = jnp.einsum('hqk,khd->qhd', soft_weights, value_rows, precision=HIGHEST).reshape(tokens, HEADS * HEAD_DIM)
    attended = low_back(low(attended))
    branch = low_back(matmul(attended, w_out))
    hidden_state = inputs + rms_norm(branch, gain_attn)
    mlp_rows = low(hidden_state)
    gate_act = low_back(matmul(mlp_rows, w_gate))
    up_proj = low_back(matmul(mlp_rows, w_up))
    mixed_rows = low(jax.nn.silu(gate_act) * up_proj)
    mlp_branch = low_back(matmul(mixed_rows, w_down))
    return hidden_state + rms_norm(mlp_branch, gain_mlp)

def add_pair(left, right):
    return left + right

def reference(inputs, segment_ids, w_query, w_key, w_value, w_out, w_gate, w_up, w_down, gain_query, gain_key, gain_attn, gain_mlp, cotangent):
    groups = inputs.shape[0] // TOK_GRP
    params = (w_query.astype(jnp.float32), w_key.astype(jnp.float32), w_value.astype(jnp.float32), w_out.astype(jnp.float32), w_gate.astype(jnp.float32), w_up.astype(jnp.float32), w_down.astype(jnp.float32), gain_query.astype(jnp.float32), gain_key.astype(jnp.float32), gain_attn.astype(jnp.float32), gain_mlp.astype(jnp.float32))
    stacked_in = inputs.astype(jnp.float32).reshape(groups, TOK_GRP, D)
    stacked_ids = segment_ids.reshape(groups, TOK_GRP)
    stacked_ct = cotangent.astype(jnp.float32).reshape(groups, TOK_GRP, D)

    def one_group(totals, pieces):
        group_in, group_ids, group_ct = pieces

        def forward(values_in, weights_in):
            return group_forward(values_in, group_ids, weights_in)
        result, pullback = jax.vjp(forward, group_in, params)
        grad_in, grad_params = pullback(group_ct)
        return (jax.tree.map(add_pair, totals, grad_params), (result, grad_in))
    zero_grads = jax.tree.map(jnp.zeros_like, params)
    totals, (results, input_grads) = lax.scan(one_group, zero_grads, (stacked_in, stacked_ids, stacked_ct))
    output = results.reshape(groups * TOK_GRP, D).astype(jnp.bfloat16)
    grad_inputs = input_grads.reshape(groups * TOK_GRP, D)
    return (output, grad_inputs, totals[0], totals[1], totals[2], totals[3], totals[4], totals[5], totals[6], totals[7], totals[8], totals[9], totals[10])
```

```python
import jax
import jax.numpy as jnp
from jax import lax
from jax.sharding import PartitionSpec as P

HEAD_DIM = 128
EPSILON = 1e-06
THETA_BASE = 500000.0


def ring_order(size):
    return list(range(0, size, 2)) + list(range(size - 1 - size % 2, 0, -2))


def ring_perms(size):
    order = ring_order(size)
    forward = [(order[i], order[(i + 1) % size]) for i in range(size)]
    return forward, [(b, a) for a, b in forward]


class Ring:
    def __init__(self, axis):
        self.axis = axis
        self.size = lax.axis_size(axis)
        self.forward, self.backward = ring_perms(self.size)
        index = lax.axis_index(axis)
        self.place = jnp.where(index % 2 == 0, index // 2, self.size - 1 - index // 2)

    def owner(self, offset):
        place = (self.place + offset) % self.size
        half = (self.size + 1) // 2
        return jnp.where(place < half, 2 * place, 2 * (self.size - 1 - place) + 1)

    def reach(self, flip):
        long, short = self.size // 2, (self.size - 1) // 2
        return (short, long) if flip else (long, short)

    def gather(self, shard, flip):
        ahead, back = self.reach(flip)
        whole = jnp.zeros((self.size, *shard.shape), shard.dtype)
        whole = lax.dynamic_update_index_in_dim(whole, shard, self.owner(0), 0)
        right = left = shard
        for hop in range(1, max(ahead, back) + 1):
            if hop <= ahead:
                right = lax.ppermute(right, self.axis, self.forward)
                whole = lax.dynamic_update_index_in_dim(whole, right, self.owner(-hop), 0)
            if hop <= back:
                left = lax.ppermute(left, self.axis, self.backward)
                whole = lax.dynamic_update_index_in_dim(whole, left, self.owner(hop), 0)
        return whole

    def scatter(self, pieces, flip):
        ahead, back = self.reach(flip)

        def own(offset):
            return lax.dynamic_index_in_dim(pieces, self.owner(offset), 0, keepdims=False)

        right, left = own(ahead), own(-back)
        for hop in range(1, max(ahead, back) + 1):
            if hop <= ahead:
                right = lax.ppermute(right, self.axis, self.forward)
                if hop < ahead:
                    right = (
                        right.astype(jnp.float32) + own(ahead - hop).astype(jnp.float32)
                    ).astype(jnp.bfloat16)
            if hop <= back:
                left = lax.ppermute(left, self.axis, self.backward)
                if hop < back:
                    left = (
                        left.astype(jnp.float32) + own(hop - back).astype(jnp.float32)
                    ).astype(jnp.bfloat16)
        return right.astype(jnp.float32) + left.astype(jnp.float32) + own(0).astype(jnp.float32)


def swap(value, bit):
    size = lax.axis_size("tensor")
    return lax.ppermute(value, "tensor", [(i, i ^ bit) for i in range(size)])


def tensor_gather(rows):
    far = swap(rows, 2)
    near = swap(rows, 1)
    return jnp.concatenate([rows, near, far, swap(far, 1)], axis=0)


def tensor_scatter(partial):
    low = partial.astype(jnp.bfloat16)
    got = swap(jnp.stack([low[1], low[3]]), 1)
    pair_far = partial[2] + got[1].astype(jnp.float32)
    far = swap(pair_far.astype(jnp.bfloat16), 2)
    return partial[0] + got[0].astype(jnp.float32) + far.astype(jnp.float32)


def tensor_total(stats):
    total = stats
    for bit in range(1, lax.axis_size("tensor")):
        other = swap(stats, bit)
        total = total + jnp.stack([other[:, b ^ bit] for b in range(stats.shape[1])], axis=1)
    return total


def dot(left, right, left_dim, right_dim):
    return lax.dot_general(
        left,
        right,
        (((left_dim,), (right_dim,)), ((), ())),
        preferred_element_type=jnp.float32,
    )


def positions(segment):
    earlier = (segment[None, :] < segment[:, None]).astype(jnp.int32)
    return jnp.arange(segment.shape[0], dtype=jnp.int32) - jnp.sum(earlier, axis=1)


def rope_tables(position, half_dim):
    frequency = THETA_BASE ** (-jnp.arange(half_dim, dtype=jnp.float32) / half_dim)
    angles = position.astype(jnp.float32)[:, None] * frequency[None, :]
    return (jnp.cos(angles), jnp.sin(angles))


def rotate(head, cosine, sine):
    half_dim = head.shape[-1] // 2
    front, back = head[:, :half_dim], head[:, half_dim:]
    return jnp.concatenate(
        [front * cosine - back * sine, back * cosine + front * sine], axis=1
    )


def norm_back(grad_normed, normed, inv_root):
    return inv_root * (grad_normed - normed * jnp.mean(grad_normed * normed, axis=1, keepdims=True))


def head_forward(query, key, value, allowed, score_scale):
    scores = dot(query, key, 1, 1) * score_scale
    scores = jnp.where(allowed, scores, -1e30)
    row_max = jnp.max(scores, axis=1, keepdims=True)
    shifted = jnp.exp(scores - row_max)
    row_total = jnp.sum(shifted, axis=1, keepdims=True)
    soft = (shifted / row_total).astype(jnp.bfloat16)
    return dot(soft, value, 1, 0).astype(jnp.bfloat16), row_max + jnp.log(row_total)


def head_backward(query, key, value, grad, log_total, allowed, score_scale):
    scores = dot(query, key, 1, 1) * score_scale
    soft = jnp.where(allowed, jnp.exp(scores - log_total), 0.0)
    weight_grad = dot(grad, value, 1, 1)
    center = jnp.sum(soft * weight_grad, axis=1, keepdims=True)
    score_grad = (soft * (weight_grad - center)).astype(jnp.bfloat16)
    query_grad = dot(score_grad, key, 1, 0) * score_scale
    key_grad = dot(score_grad, query, 0, 0) * score_scale
    value_grad = dot(soft.astype(jnp.bfloat16), grad, 0, 0).astype(jnp.bfloat16)
    return query_grad, key_grad, value_grad


def shards(
    inputs,
    segment_ids,
    w_query,
    w_key,
    w_value,
    w_out,
    w_gate,
    w_up,
    w_down,
    gain_query,
    gain_key,
    gain_attn,
    gain_mlp,
    cotangent,
):
    f32, bf16 = jnp.float32, jnp.bfloat16
    rows, dim_model = inputs.shape
    width = w_query.shape[1]
    heads = width // HEAD_DIM
    group_len = segment_ids.shape[0]
    blocks = group_len // rows
    score_scale = HEAD_DIM ** (-0.5)
    tensor_index = lax.axis_index("tensor")
    offset = tensor_index * width
    ring = Ring("dp")

    flat = lambda whole: whole.reshape(dim_model, whole.shape[-1])
    w_qkv = flat(ring.gather(jnp.concatenate([w_query, w_key, w_value], axis=1), False))
    tokens = tensor_gather(inputs)
    out_t = flat(ring.gather(w_out.T, True))
    gate_w = flat(ring.gather(w_gate, False))
    up_w = flat(ring.gather(w_up, True))
    down_t = flat(ring.gather(w_down.T, False))

    block_ids = tensor_index ^ jnp.arange(blocks, dtype=jnp.int32)
    reorder = lambda v: jnp.take(v.reshape(blocks, rows), block_ids, axis=0).reshape(group_len)
    position = reorder(positions(segment_ids))
    segment = reorder(segment_ids)
    order = reorder(jnp.arange(group_len, dtype=jnp.int32))
    cosine, sine = rope_tables(position, HEAD_DIM // 2)
    allowed = (segment[None, :] == segment[:, None]) & (order[None, :] <= order[:, None])

    qkv = dot(tokens, w_qkv, 1, 0)
    query_raw, key_raw = qkv[:, :width], qkv[:, width : 2 * width]
    value_rows = qkv[:, 2 * width :].astype(bf16)
    row_sums = lambda *products: tensor_total(
        jnp.stack([jnp.sum(v, axis=1) for v in products]).reshape(len(products), blocks, rows)
    ).reshape(len(products), group_len)
    totals = row_sums(query_raw * query_raw, key_raw * key_raw)
    query_inv = lax.rsqrt(totals[0] / dim_model + EPSILON)[:, None]
    key_inv = lax.rsqrt(totals[1] / dim_model + EPSILON)[:, None]
    query_gain = lax.dynamic_slice_in_dim(gain_query, offset, width)
    key_gain = lax.dynamic_slice_in_dim(gain_key, offset, width)
    query_hat = query_raw * query_inv
    key_hat = key_raw * key_inv

    head_of = lambda v, h: v[:, h * HEAD_DIM : (h + 1) * HEAD_DIM]
    query_in, key_in = query_hat * query_gain, key_hat * key_gain
    queries = [rotate(head_of(query_in, h), cosine, sine).astype(bf16) for h in range(heads)]
    keys = [rotate(head_of(key_in, h), cosine, sine).astype(bf16) for h in range(heads)]
    values = [head_of(value_rows, h) for h in range(heads)]
    head_out, log_totals = zip(
        *[head_forward(queries[h], keys[h], values[h], allowed, score_scale) for h in range(heads)]
    )
    attended = jnp.concatenate(head_out, axis=1)
    branch = tensor_scatter(dot(attended, out_t, 1, 1).reshape(blocks, rows, dim_model))
    branch_inv = lax.rsqrt(jnp.mean(branch * branch, axis=1, keepdims=True) + EPSILON)
    branch_hat = branch * branch_inv
    hidden_state = inputs.astype(f32) + branch_hat * gain_attn
    mlp_rows = tensor_gather(hidden_state.astype(bf16))
    gate_act = dot(mlp_rows, gate_w, 1, 0)
    up_proj = dot(mlp_rows, up_w, 1, 0)
    gate_sigmoid = jax.nn.sigmoid(gate_act)
    mixed_rows = (gate_act * gate_sigmoid * up_proj).astype(bf16)
    mlp_branch = tensor_scatter(dot(mixed_rows, down_t, 1, 1).reshape(blocks, rows, dim_model))
    mlp_inv = lax.rsqrt(jnp.mean(mlp_branch * mlp_branch, axis=1, keepdims=True) + EPSILON)
    mlp_hat = mlp_branch * mlp_inv
    output = (hidden_state + mlp_hat * gain_mlp).astype(bf16)

    upstream = cotangent.astype(f32)
    gain_mlp_grad = jnp.sum(upstream * mlp_hat, axis=0)
    mlp_grad = norm_back(upstream * gain_mlp, mlp_hat, mlp_inv).astype(bf16)
    grad_rows = tensor_gather(mlp_grad)
    pieces = lambda g: g.astype(bf16).reshape(ring.size, dim_model // ring.size, g.shape[-1])
    down_sum = ring.scatter(pieces(dot(grad_rows, mixed_rows, 0, 0)), False).T
    mixed_grad = dot(grad_rows, down_t, 1, 0)
    gate_grad = (
        mixed_grad * up_proj * gate_sigmoid * (1.0 + gate_act * (1.0 - gate_sigmoid))
    ).astype(bf16)
    up_grad = (mixed_grad * gate_act * gate_sigmoid).astype(bf16)
    gate_sum = ring.scatter(pieces(dot(mlp_rows, gate_grad, 0, 0)), True)
    up_sum = ring.scatter(pieces(dot(mlp_rows, up_grad, 0, 0)), False)
    hidden_partial = dot(gate_grad, gate_w, 1, 1) + dot(up_grad, up_w, 1, 1)
    hidden_grad = upstream + tensor_scatter(hidden_partial.reshape(blocks, rows, dim_model))
    gain_attn_grad = jnp.sum(hidden_grad * branch_hat, axis=0)
    branch_grad = norm_back(hidden_grad * gain_attn, branch_hat, branch_inv).astype(bf16)
    attn_grad_rows = tensor_gather(branch_grad)
    out_sum = ring.scatter(pieces(dot(attn_grad_rows, attended, 0, 0)), True).T
    attended_grad = dot(attn_grad_rows, out_t, 1, 0).astype(bf16)

    query_grads, key_grads, value_grads = zip(
        *[
            head_backward(
                queries[h],
                keys[h],
                values[h],
                head_of(attended_grad, h),
                log_totals[h],
                allowed,
                score_scale,
            )
            for h in range(heads)
        ]
    )
    query_norm_grad = jnp.concatenate([rotate(g, cosine, -sine) for g in query_grads], axis=1)
    key_norm_grad = jnp.concatenate([rotate(g, cosine, -sine) for g in key_grads], axis=1)
    query_hat_grad = query_norm_grad * query_gain
    key_hat_grad = key_norm_grad * key_gain
    dots = row_sums(query_hat_grad * query_hat, key_hat_grad * key_hat)
    query_raw_grad = query_inv * (query_hat_grad - query_hat * (dots[0] / dim_model)[:, None])
    key_raw_grad = key_inv * (key_hat_grad - key_hat * (dots[1] / dim_model)[:, None])
    qkv_grad = jnp.concatenate(
        [query_raw_grad.astype(bf16), key_raw_grad.astype(bf16), *value_grads], axis=1
    )
    qkv_sum = ring.scatter(pieces(dot(tokens, qkv_grad, 0, 0)), False)
    input_partial = dot(qkv_grad, w_qkv, 1, 1)
    input_grad = hidden_grad + tensor_scatter(input_partial.reshape(blocks, rows, dim_model))

    own_part = lambda v: lax.dynamic_update_slice_in_dim(
        jnp.zeros((dim_model,), f32), jnp.sum(v, axis=0), offset, 0
    )
    gains = lax.psum(
        jnp.stack(
            [
                own_part(query_norm_grad * query_hat),
                own_part(key_norm_grad * key_hat),
                gain_attn_grad,
                gain_mlp_grad,
            ]
        ),
        ("dp", "tensor"),
    )
    return (
        output,
        input_grad,
        qkv_sum[:, :width],
        qkv_sum[:, width : 2 * width],
        qkv_sum[:, 2 * width :],
        out_sum,
        gate_sum,
        up_sum,
        down_sum,
        gains[0],
        gains[1],
        gains[2],
        gains[3],
    )


def solution(mesh):
    tokens_placed = P(("dp", "tensor"), None)
    columns, down = P("dp", "tensor"), P("tensor", "dp")
    weights = (columns, columns, columns, down, columns, columns, down)
    return jax.shard_map(
        shards,
        mesh=mesh,
        in_specs=(tokens_placed, P("dp"), *weights, P(), P(), P(), P(), tokens_placed),
        out_specs=(tokens_placed, tokens_placed, *weights, P(), P(), P(), P()),
        check_vma=False,
    )
```
